256 devices in a mesh: feat: 32 (over y, z), dp: 8 (over x, core).
Axes of the slice: x: 4, y: 4, z: 8, core: 2. Of those that a mesh axis runs over, the one named last changes fastest.
Arguments:
- face_grid: bfloat16 [32768, 10240], P('dp', 'feat'), may hold values from -6 to 6
- first_nbrs: int32 [16384, 8], P('dp'), may hold values from 0 to 4095
- first_count: int32 [16384], P('dp'), may hold values from 1 to 8
- w_first: bfloat16 [10240, 256], P('feat'), may hold values from -0.0625 to 0.0625
- b_first: float32 [256], replicated, may hold values from -3 to 3
- send_rows: int32 [4096], P('dp'), may hold values from 0 to 2047
- second_nbrs: int32 [16384, 8], P(('dp', 'feat')), may hold values from 0 to 2559
- second_count: int32 [16384], P(('dp', 'feat')), may hold values from 1 to 8
- w_in: bfloat16 [256, 1024], replicated, may hold values from -0.375 to 0.375
- w_out: bfloat16 [1024, 256], replicated, may hold values from -0.1875 to 0.1875
- out_grad: bfloat16 [16384, 256], P(('dp', 'feat')), may hold values from -6 to 6
Outputs:
- embed: bfloat16 [16384, 256], P(('dp', 'feat'))
- grad_first: float32 [10240, 256], P('feat')
The draws below stay inside these ranges and needn't reach their ends.
Inputs may be any that keep to these rules, and one draw needn't show every extreme that they name: `first_count`: slots at or past a target's count are ignored; counts lie in 1 to 8. `first_nbrs`: only slots below first_count are read. `second_count`: slots at or past a target's count are ignored. `second_nbrs`: indices below 2048 name the partition's own targets, the rest the faces received from the previous partition in order; only slots below second_count are read. `send_rows`: entries may repeat.
All inputs are finite; a program needn't handle non-finite values.
Results may differ from the reference program's by a relative error of at most 0.0061.
Values may be sent and summed in bfloat16 or wider, within the bound.
No kernel may reach another device: no remote copies, remote signals or barrier semaphores. Data moves between devices by JAX's collectives and lax.ppermute only.
A program may use at most 64 MiB of HBM per device.

```python
import jax
import jax.numpy as jnp
from jax import lax

F = 10240
HID = 256
MLP = 1024
K = 8
G = 2048
SRC = 4096
HALO = 512
N_DP = 8


def plant(values, rng, least, largest):
    spot = [jax.random.randint(jax.random.fold_in(rng, axis), (), 0, length) for axis, length in enumerate(values.shape)]
    widest = values.shape.index(max(values.shape))
    neighbour = spot[:widest] + [(spot[widest] + 1) % values.shape[widest]] + spot[widest + 1:]
    return values.at[tuple(spot)].set(least).at[tuple(neighbour)].set(largest)


def block_levels(own_key, extent, pieces, smallest, high):
    gain, own = 1.0, jax.random.fold_in(own_key, 6)
    for position, blocks in pieces:
        draws = jnp.exp(jax.random.uniform(jax.random.fold_in(own, position), (blocks,), jnp.float32, smallest / len(pieces), high / len(pieces)))
        gain = gain * jnp.repeat(draws, extent[position] // blocks).reshape([-1 if axis == position else 1 for axis in range(len(extent))])
    return gain


def gaussian(stream_key, extent, scale, limit, cuts=(), kind=jnp.bfloat16):
    array = scale * jax.random.normal(stream_key, extent, jnp.float32)
    if cuts:
        array = array * block_levels(stream_key, extent, cuts, -0.22, 0.18)
    return jnp.clip(array, -limit, limit).astype(kind)


def setup_inputs(seed: int = 0) -> dict:
    seeds = jax.random.split(jax.random.key(seed), 12)
    return {
        "face_grid": gaussian(seeds[0], (N_DP * SRC, F), 1.0, 6.0, ((0, 8), (1, 32))),
        "first_nbrs": plant(jax.random.randint(seeds[1], (N_DP * G, K), 0, SRC), jax.random.fold_in(seeds[1], 1), 0, SRC - 1).astype(jnp.int32),
        "first_count": plant(jax.random.randint(seeds[2], (N_DP * G,), 1, K + 1), jax.random.fold_in(seeds[2], 1), 1, K).astype(jnp.int32),
        "w_first": gaussian(seeds[3], (F, HID), F ** -0.5, 0.0625, ((0, 32),)),
        "b_first": gaussian(seeds[4], (HID,), 0.5, 3.0, (), jnp.float32),
        "send_rows": plant(jax.random.randint(seeds[5], (N_DP * HALO,), 0, G), jax.random.fold_in(seeds[5], 1), 0, G - 1).astype(jnp.int32),
        "second_nbrs": plant(jax.random.randint(seeds[6], (N_DP * G, K), 0, G + HALO), jax.random.fold_in(seeds[6], 1), 0, (G + HALO) - 1).astype(jnp.int32),
        "second_count": plant(jax.random.randint(seeds[7], (N_DP * G,), 1, K + 1), jax.random.fold_in(seeds[7], 1), 1, K).astype(jnp.int32),
        "w_in": gaussian(seeds[8], (HID, MLP), HID ** -0.5, 0.375),
        "w_out": gaussian(seeds[9], (MLP, HID), MLP ** -0.5, 0.1875),
        "out_grad": gaussian(seeds[10], (N_DP * G, HID), 1.0, 6.0, ((0, 256),)),
    }


def slope(value):
    sig = jax.nn.sigmoid(value)
    return sig * (1.0 + value * (1.0 - sig))


def mean_rows(table, nbrs, count):
    total = jnp.zeros((nbrs.shape[0], table.shape[1]), jnp.float32)
    for slot in range(nbrs.shape[1]):
        picked = table[nbrs[:, slot]].astype(jnp.float32)
        total = total + jnp.where((slot < count)[:, None], picked, 0.0)
    return total / count[:, None].astype(jnp.float32)


def spread(grad, nbrs, count, size):
    slots = jnp.arange(nbrs.shape[1], dtype=jnp.int32)
    factor = jnp.where(slots[None, :] < count[:, None], 1.0 / count[:, None].astype(jnp.float32), 0.0)
    terms = (grad[:, None, :] * factor[:, :, None]).reshape(-1, grad.shape[1])
    return jax.ops.segment_sum(terms, nbrs.reshape(-1), num_segments=size)


def reference(face_grid, first_nbrs, first_count, w_first, b_first, send_rows, second_nbrs, second_count, w_in, w_out, out_grad):
    agg_list, pre_list, hid_list = [], [], []
    for part in range(N_DP):
        sources = face_grid[part * SRC:(part + 1) * SRC]
        nbrs = first_nbrs[part * G:(part + 1) * G]
        count = first_count[part * G:(part + 1) * G]
        agg = (sources[:G].astype(jnp.float32) + mean_rows(sources, nbrs, count)).astype(jnp.bfloat16)
        pre = jnp.dot(agg, w_first, preferred_element_type=jnp.float32) + b_first
        agg_list.append(agg)
        pre_list.append(pre)
        hid_list.append(jax.nn.silu(pre).astype(jnp.bfloat16))
    embeds, grad_aggs, grad_exts = [], [], []
    for part in range(N_DP):
        prev = (part - 1) % N_DP
        sent = hid_list[prev][send_rows[prev * HALO:(prev + 1) * HALO]]
        extended = jnp.concatenate([hid_list[part], sent], axis=0)
        nbrs = second_nbrs[part * G:(part + 1) * G]
        count = second_count[part * G:(part + 1) * G]
        agg2 = (hid_list[part].astype(jnp.float32) + mean_rows(extended, nbrs, count)).astype(jnp.bfloat16)
        pre_mlp = jnp.dot(agg2, w_in, preferred_element_type=jnp.float32)
        act = jax.nn.silu(pre_mlp).astype(jnp.bfloat16)
        embeds.append((hid_list[part].astype(jnp.float32) + jnp.dot(act, w_out, preferred_element_type=jnp.float32)).astype(jnp.bfloat16))
        cot = out_grad[part * G:(part + 1) * G]
        grad_act = lax.dot_general(cot, w_out, (((1,), (1,)), ((), ())), preferred_element_type=jnp.float32)
        grad_pre = (grad_act * slope(pre_mlp)).astype(jnp.bfloat16)
        grad_agg = lax.dot_general(grad_pre, w_in, (((1,), (1,)), ((), ())), preferred_element_type=jnp.float32)
        grad_aggs.append(grad_agg)
        grad_exts.append(spread(grad_agg, nbrs, count, G + HALO))
    grad_first = jnp.zeros((F, HID), jnp.float32)
    for part in range(N_DP):
        nxt = (part + 1) % N_DP
        cot = out_grad[part * G:(part + 1) * G].astype(jnp.float32)
        table_grad = grad_exts[part][:G].at[send_rows[part * HALO:(part + 1) * HALO]].add(grad_exts[nxt][G:])
        grad_hidden = cot + grad_aggs[part] + table_grad
        grad_pre = (grad_hidden * slope(pre_list[part])).astype(jnp.bfloat16)
        grad_first = grad_first + lax.dot_general(agg_list[part], grad_pre, (((0,), (0,)), ((), ())), preferred_element_type=jnp.float32)
    return jnp.concatenate(embeds, axis=0), grad_first
```

```python
import jax
import jax.numpy as jnp
from jax import lax
from jax.experimental import pallas as pl
from jax.experimental.pallas import tpu as pltpu
from jax.sharding import Mesh, PartitionSpec as P

BF = jnp.bfloat16
F32 = jnp.float32
NY, NZ = 4, 8
BLOCK = 512


def count_rows(idx, mult, base, rows):
    slots, width = idx.shape
    local = idx - base
    cols = [jnp.broadcast_to(local[k : k + 1, :], (16, width)).astype(BF) for k in range(slots)]
    vals = [jnp.broadcast_to(mult[k : k + 1, :], (16, width)).astype(BF) for k in range(slots)]
    row = lax.broadcasted_iota(jnp.int32, (16, width), 0).astype(F32)
    out = []
    for group in range(rows // 16):
        here = (row + float(16 * group)).astype(BF)
        acc = jnp.zeros((16, width), BF)
        for k in range(slots):
            acc = jnp.where(here == cols[k], vals[k], acc)
        out.append(acc)
    return jnp.concatenate(out, axis=0)


def agg_body(block_ref, face_ref, idx_ref, mult_ref, inv_ref, w_ref, agg_ref, part_ref):
    width = agg_ref.shape[1]
    idx, mult = idx_ref[...], mult_ref[...]
    total = jnp.zeros(agg_ref.shape, F32)
    for j in range(face_ref.shape[1] // 256):
        counts = count_rows(idx, mult, float(256 * j), 256)
        total = total + jnp.dot(
            face_ref[:, 256 * j : 256 * (j + 1)], counts, preferred_element_type=F32
        )
    start = pl.multiple_of(block_ref[0] * width, width)
    own = face_ref[:, pl.ds(start, width)].astype(F32)
    agg = (own + total * inv_ref[...]).astype(BF)
    agg_ref[...] = agg
    part_ref[...] = jnp.dot(w_ref[...], agg, preferred_element_type=F32).astype(BF)


def agg_chunk(block, face_t, idx, mult, inv, w_t):
    feats, sources = face_t.shape
    hid = w_t.shape[0]
    spec = pltpu.PrefetchScalarGridSpec(
        num_scalar_prefetch=1,
        grid=(1,),
        in_specs=[
            pl.BlockSpec((feats, sources), lambda i, b: (0, 0)),
            pl.BlockSpec((8, BLOCK), lambda i, b: (0, b[0])),
            pl.BlockSpec((8, BLOCK), lambda i, b: (0, b[0])),
            pl.BlockSpec((1, BLOCK), lambda i, b: (0, b[0])),
            pl.BlockSpec((hid, feats), lambda i, b: (0, 0)),
        ],
        out_specs=[
            pl.BlockSpec((feats, BLOCK), lambda i, b: (0, 0)),
            pl.BlockSpec((hid, BLOCK), lambda i, b: (0, 0)),
        ],
    )
    return pl.pallas_call(
        agg_body,
        grid_spec=spec,
        out_shape=[
            jax.ShapeDtypeStruct((feats, BLOCK), BF),
            jax.ShapeDtypeStruct((hid, BLOCK), BF),
        ],
        cost_estimate=pl.CostEstimate(
            flops=2 * BLOCK * feats * (sources + hid), bytes_accessed=4 << 20, transcendentals=0
        ),
        name="agg_chunk",
    )(block, face_t, idx, mult, inv, w_t)


def count_body(idx_ref, mult_ref, out_ref):
    rows, width = out_ref.shape
    base = (pl.program_id(0) * rows).astype(F32)
    for c in range(width // 512):
        cut = slice(512 * c, 512 * (c + 1))
        out_ref[:, cut] = count_rows(idx_ref[:, cut], mult_ref[:, cut], base, rows)


def count_matrix(idx, mult, rows):
    slots, width = idx.shape
    step = 256
    return pl.pallas_call(
        count_body,
        grid=(rows // step,),
        in_specs=[pl.BlockSpec((slots, width), lambda i: (0, 0))] * 2,
        out_specs=pl.BlockSpec((step, width), lambda i: (i, 0)),
        out_shape=jax.ShapeDtypeStruct((rows, width), BF),
        name="count_matrix",
    )(idx, mult)


def live_slots(nbrs_t, count):
    slots = jnp.arange(nbrs_t.shape[0], dtype=jnp.int32)[:, None]
    idx = jnp.where(slots < count[None, :], nbrs_t, -1)
    mult = sum((idx == idx[k : k + 1]).astype(F32) for k in range(nbrs_t.shape[0]))
    return idx.astype(F32), mult


def shift(value, axis, by):
    devices = lax.axis_size(axis)
    return lax.ppermute(value, axis, [(i, (i + by) % devices) for i in range(devices)])


def swap(value, axis, bit):
    return lax.ppermute(value, axis, [(i, i ^ bit) for i in range(lax.axis_size(axis))])


def gather_z(piece):
    wide = jnp.broadcast_to(piece[None], (NZ,) + piece.shape)
    return lax.all_to_all(wide, "z", 0, 0).reshape(NZ * piece.shape[0], piece.shape[1])


def gather_y(own):
    return [own] + [shift(own, "y", NY - d) for d in range(1, NY)]


def slope(value):
    sig = jax.nn.sigmoid(value)
    return sig * (1.0 + value * (1.0 - sig))


def dot_nn(a, b):
    return lax.dot_general(a, b, (((1,), (0,)), ((), ())), preferred_element_type=F32)


def dot_nt(a, b):
    return lax.dot_general(a, b, (((1,), (1,)), ((), ())), preferred_element_type=F32)


def dot_tn(a, b):
    return lax.dot_general(a, b, (((0,), (0,)), ((), ())), preferred_element_type=F32)


def body(
    face_grid,
    first_nbrs,
    first_count,
    w_first,
    b_first,
    send_rows,
    second_nbrs,
    second_count,
    w_in,
    w_out,
    out_grad,
):
    y, z = lax.axis_index("y"), lax.axis_index("z")
    core = lax.axis_index("core")
    targets = first_nbrs.shape[0]
    hid = w_first.shape[1]
    halo = send_rows.shape[0]

    packed = jnp.concatenate(
        [
            out_grad,
            (second_nbrs >> 8).astype(BF),
            (second_nbrs & 255).astype(BF),
            second_count[:, None].astype(BF),
            jnp.zeros((out_grad.shape[0], 111), BF),
        ],
        axis=1,
    )
    whole = jnp.concatenate(gather_y(gather_z(packed)), axis=0)
    cot = whole[:, :hid]
    lists = whole[:, hid : hid + 17].astype(F32).astype(jnp.int32).T
    nbrs2 = lists[0:8] * 256 + lists[8:16]
    count2 = lists[16]
    turn = y * BLOCK
    nbrs2 = jnp.where(nbrs2 < targets, (nbrs2 - turn) & (targets - 1), nbrs2)
    idx2, mult2 = live_slots(nbrs2, count2)
    inv2 = 1.0 / count2[None, :].astype(F32)
    mat = count_matrix(idx2, mult2, targets + halo)
    rows = ((send_rows - turn) & (targets - 1)).astype(F32)[None, :]
    pick = count_matrix(rows, jnp.ones_like(rows), targets)

    face_t = face_grid.T
    w_first_t = w_first.T
    idx1, mult1 = live_slots(first_nbrs.T, first_count)
    inv1 = 1.0 / first_count[None, :].astype(F32)
    agg, got = {}, []
    for d in (2, 1, 3, 0):
        block = ((y + d) % NY).astype(jnp.int32).reshape(1)
        agg[d], part = agg_chunk(block, face_t, idx1, mult1, inv1, w_first_t)
        got.append(part if d == 0 else shift(part, "y", d))
    part_y = sum(g.astype(F32) for g in got).astype(BF)
    by_z = lax.all_to_all(part_y.reshape(NZ, hid // NZ, BLOCK), "z", 0, 0)
    bias = lax.dynamic_slice(b_first, (z * (hid // NZ),), (hid // NZ,))
    pre_own = jnp.sum(by_z.astype(F32), axis=0) + bias[:, None]
    pre = jnp.concatenate(gather_y(gather_z(pre_own.astype(BF))), axis=1).astype(F32)
    hidden = jax.nn.silu(pre).astype(BF)

    sent = dot_nn(hidden, pick).astype(BF)
    received = shift(sent, ("x", "core"), 1)
    total = dot_nn(hidden, mat[:targets]) + dot_nn(received, mat[targets:])
    agg2 = (hidden.astype(F32) + total * inv2).astype(BF)
    pre_mlp = dot_tn(w_in, agg2)
    grad_act = dot_nt(w_out, cot)
    grad_pre = (grad_act * slope(pre_mlp)).astype(BF)
    grad_agg = dot_nn(w_in, grad_pre)
    shared = (grad_agg * inv2).astype(BF)
    back = dot_nt(shared, mat[targets:]).astype(BF)
    returned = shift(back, ("x", "core"), -1)
    grad_table = dot_nt(shared, mat[:targets]) + dot_nt(returned, pick)
    grad_hidden = cot.T.astype(F32) + grad_agg + grad_table
    grad_first_pre = (grad_hidden * slope(pre)).astype(BF)
    slice_grad = sum(
        dot_nt(agg[d], grad_first_pre[:, BLOCK * d : BLOCK * (d + 1)]) for d in range(NY)
    )

    first = z * (BLOCK // NZ)
    own_mlp = lax.dynamic_slice(pre_mlp, (0, first), (pre_mlp.shape[0], BLOCK // NZ))
    own_hidden = lax.dynamic_slice(hidden, (0, first), (hid, BLOCK // NZ))
    act = jax.nn.silu(own_mlp).astype(BF)
    embed = (own_hidden.T.astype(F32) + dot_tn(act, w_out)).astype(BF)

    half = slice_grad.shape[0] // 2
    low, high = slice_grad[:half], slice_grad[half:]
    keep = jnp.where(core == 0, low, high)
    give = jnp.where(core == 0, high, low)
    pair = (keep + swap(give, "core", 1)).astype(BF)
    one, two, three = (swap(pair, "x", bit).astype(F32) for bit in (1, 2, 3))
    done = (pair.astype(F32) + one) + (two + three)
    other = swap(done, "core", 1)
    grad_first = jnp.concatenate(
        [jnp.where(core == 0, done, other), jnp.where(core == 0, other, done)], axis=0
    )
    return embed, grad_first


def solution(mesh):
    fine = Mesh(mesh.devices.reshape(NY, NZ, 4, 2), ("y", "z", "x", "core"))
    feat, dp, every = ("y", "z"), ("x", "core"), ("x", "core", "y", "z")
    return jax.shard_map(
        body,
        mesh=fine,
        in_specs=(
            P(dp, feat),
            P(dp, None),
            P(dp),
            P(feat, None),
            P(),
            P(dp),
            P(every, None),
            P(every),
            P(),
            P(),
            P(every, None),
        ),
        out_specs=(P(every, None), P(feat, None)),
        check_vma=False,
    )
```

```python
import functools

import jax
import jax.numpy as jnp
from jax import lax
from jax.experimental import pallas as pl
from jax.experimental.pallas import tpu as pltpu
from jax.sharding import Mesh, PartitionSpec as P


BF = jnp.bfloat16
F32 = jnp.float32
NY, NZ = 4, 8
BLOCK = 512
PIECE = BLOCK // NZ


def dot_nn(a, b):
    return lax.dot_general(a, b, (((1,), (0,)), ((), ())), preferred_element_type=F32)


def dot_nt(a, b):
    return lax.dot_general(a, b, (((1,), (1,)), ((), ())), preferred_element_type=F32)


def dot_tn(a, b):
    return lax.dot_general(a, b, (((0,), (0,)), ((), ())), preferred_element_type=F32)


def slope(value):
    half = 0.5 * jnp.tanh(0.5 * value)
    sig = 0.5 + half
    return sig * (1.0 + value * (0.5 - half))


def live_slots(nbrs, count):
    slot = lax.broadcasted_iota(jnp.int32, nbrs.shape, 0)
    idx = jnp.where(slot < count, nbrs, -1).astype(F32)
    mult = sum(jnp.where(idx == idx[k : k + 1], 1.0, 0.0) for k in range(nbrs.shape[0]))
    return idx, mult


def count_rows(idx, mult, base, rows):
    slots, width = idx.shape
    local = idx - base
    cols = [jnp.broadcast_to(local[k : k + 1, :], (16, width)).astype(BF) for k in range(slots)]
    vals = [jnp.broadcast_to(mult[k : k + 1, :], (16, width)).astype(BF) for k in range(slots)]
    row = lax.broadcasted_iota(jnp.int32, (16, width), 0).astype(F32)
    out = []
    for group in range(rows // 16):
        here = (row + float(16 * group)).astype(BF)
        acc = jnp.zeros((16, width), BF)
        for k in range(slots):
            acc = jnp.where(here == cols[k], vals[k], acc)
        out.append(acc)
    return jnp.concatenate(out, axis=0)


def whole(shape):
    return pl.BlockSpec(shape, lambda *_: (0,) * len(shape))


def grant(mib):
    return pltpu.CompilerParams(vmem_limit_bytes=mib << 20)


def cost(flops, moved):
    return pl.CostEstimate(flops=flops, bytes_accessed=moved, transcendentals=0)


def aggregate(block, face_ref, nbrs, count, w, ready, agg_ref, part_ref):
    width = agg_ref.shape[1]
    idx, mult = live_slots(nbrs, count)
    steps = face_ref.shape[1] // 512

    def half(h, total):
        for j in range(steps):
            at = 256 * (h * steps + j)
            counts = count_rows(idx, mult, at.astype(F32), 256)
            ready(h, 256 * j)
            faces = face_ref[:, pl.ds(pl.multiple_of(at, 256), 256)]
            total = total + dot_nn(faces, counts)
        return total

    total = lax.fori_loop(0, 2, half, jnp.zeros(agg_ref.shape, F32))
    start = pl.multiple_of(block * width, width)
    own = face_ref[:, pl.ds(start, width)].astype(F32)
    agg = (own + total * (1.0 / count.astype(F32))).astype(BF)
    agg_ref[...] = agg
    part_ref[...] = dot_tn(w, agg).astype(BF)


PIECES = 4


def chunk_body(block_ref, face_hbm, nbrs_hbm, count_hbm, w_hbm, *refs):
    outs, (face_ref, nbrs_ref, count_ref, w_ref, sems) = refs[:-5], refs[-5:]
    width = face_ref.shape[1] // PIECES
    small = [
        pltpu.make_async_copy(nbrs_hbm, nbrs_ref, sems.at[PIECES]),
        pltpu.make_async_copy(count_hbm, count_ref, sems.at[PIECES + 1]),
        pltpu.make_async_copy(w_hbm, w_ref, sems.at[PIECES + 2]),
    ]

    def big(i):
        cut = pl.ds(pl.multiple_of(i * width, width), width)
        return pltpu.make_async_copy(face_hbm.at[:, cut], face_ref.at[:, cut], sems.at[i])

    for copy in small + [big(i) for i in range(PIECES)]:
        copy.start()
    for copy in small:
        copy.wait()

    for i in range(len(outs) // 2):

        def ready(h, at):
            if i == 0 and at % width == 0:
                big(h * (PIECES // 2) + at // width).wait()

        block = block_ref[i]
        cut = pl.ds(pl.multiple_of(block * BLOCK, BLOCK), BLOCK)
        aggregate(
            block, face_ref, nbrs_ref[:, cut], count_ref[:, cut], w_ref[...], ready,
            outs[2 * i], outs[2 * i + 1],
        )


def agg_chunk(blocks, inputs):
    feats, hid = inputs[3].shape
    out = [((feats, BLOCK), BF), ((hid, BLOCK), BF)] * blocks.shape[0]
    spec = pltpu.PrefetchScalarGridSpec(
        num_scalar_prefetch=1,
        grid=(1,),
        in_specs=[pl.BlockSpec(memory_space=pltpu.HBM)] * len(inputs),
        out_specs=[whole(shape) for shape, _ in out],
        scratch_shapes=[pltpu.VMEM(v.shape, v.dtype) for v in inputs]
        + [pltpu.SemaphoreType.DMA((PIECES + 3,))],
    )
    work = 2 * BLOCK * feats * (inputs[0].shape[1] + hid) * blocks.shape[0]
    return pl.pallas_call(
        chunk_body,
        grid_spec=spec,
        out_shape=[jax.ShapeDtypeStruct(*v) for v in out],
        compiler_params=grant(60),
        cost_estimate=cost(work, 4 << 20),
        name="agg_chunk",
    )(blocks, *inputs)


def count_body(nbrs_ref, count_ref, out_ref, *, first):
    rows, width = out_ref.shape
    base = (first + pl.program_id(0) * rows).astype(F32)

    def step(c, carry):
        cut = pl.ds(pl.multiple_of(c * BLOCK, BLOCK), BLOCK)
        idx, mult = live_slots(nbrs_ref[:, cut], count_ref[:, cut])
        out_ref[:, cut] = count_rows(idx, mult, base, rows)
        return carry

    lax.fori_loop(0, width // BLOCK, step, 0)


def count_matrix(nbrs, count, first, rows, mib=12, step=256):
    slots, width = nbrs.shape
    return pl.pallas_call(
        functools.partial(count_body, first=first),
        grid=(rows // step,),
        in_specs=[whole((slots, width)), whole((1, width))],
        out_specs=pl.BlockSpec((step, width), lambda i: (i, 0)),
        out_shape=jax.ShapeDtypeStruct((rows, width), BF),
        compiler_params=grant(mib),
        cost_estimate=cost(slots * rows * width * 200, 2 * rows * width),
        name="count_matrix",
    )(nbrs, count)


def pack_body(nbrs_ref, count_ref, out_ref):
    nbrs = nbrs_ref[...]
    count = jnp.broadcast_to(count_ref[...], nbrs.shape)
    rows = jnp.concatenate([nbrs >> 8, nbrs & 255, count, jnp.zeros_like(nbrs)], axis=1)
    rows = jnp.concatenate([rows, jnp.zeros_like(rows)], axis=0).astype(F32).astype(BF)
    out_ref[...] = jnp.concatenate([rows, jnp.zeros_like(rows)], axis=1)


def pack(nbrs_t, count):
    shape = (16, BLOCK)
    return pl.pallas_call(
        pack_body,
        in_specs=[whole(v.shape) for v in (nbrs_t, count)],
        out_specs=whole(shape),
        grid=(1,),
        out_shape=jax.ShapeDtypeStruct(shape, BF),
        compiler_params=grant(12),
        name="pack",
    )(nbrs_t, count)


def unpack_body(y_ref, *refs):
    nbrs_ref, count_ref = refs[NY:]
    targets = nbrs_ref.shape[1]
    nbrs, count = [], []
    for d in range(NY):
        for z in range(NZ):
            rows = refs[d][z].astype(F32)[:8].astype(jnp.int32)
            nbrs.append(rows[:, :PIECE] * 256 + rows[:, PIECE : 2 * PIECE])
            count.append(rows[0:1, 2 * PIECE : 3 * PIECE])
    nbrs = jnp.concatenate(nbrs, axis=1)
    turned = (nbrs - y_ref[0] * BLOCK) & (targets - 1)
    nbrs_ref[...] = jnp.where(nbrs < targets, turned, nbrs)
    count_ref[...] = jnp.concatenate(count, axis=1)


def unpack(y, blocks):
    targets = NY * NZ * PIECE
    out = [((8, targets), jnp.int32), ((1, targets), jnp.int32)]
    spec = pltpu.PrefetchScalarGridSpec(
        num_scalar_prefetch=1,
        grid=(1,),
        in_specs=[whole(v.shape) for v in blocks],
        out_specs=[whole(shape) for shape, _ in out],
    )
    return pl.pallas_call(
        unpack_body,
        grid_spec=spec,
        out_shape=[jax.ShapeDtypeStruct(*v) for v in out],
        compiler_params=grant(12),
        name="unpack",
    )(y, *blocks)


def mlp_body(
    total_ref, received_ref, mat_ref, hidden_ref, count_ref, cot_ref, w_in_t_ref, w_in_ref, w_out_ref,
    agg_ref, grad_ref, shared_ref, back_ref, acc_ref,
):
    step = pl.program_id(0)
    inv = 1.0 / count_ref[...].astype(F32)
    total = total_ref[...] + dot_nn(received_ref[...], mat_ref[...])
    agg = (hidden_ref[...].astype(F32) + total * inv).astype(BF)

    @pl.when(step == 0)
    def _():
        agg_ref[...] = agg

    cot = cot_ref[...]
    grad = None
    inner = w_in_ref.shape[1] // 2
    for m in range(2):
        cut = slice(inner * m, inner * (m + 1))
        pre = dot_nn(w_in_t_ref[cut, :], agg)
        grad_act = dot_nt(w_out_ref[cut, :], cot)
        grad_pre = (grad_act * slope(pre)).astype(BF)
        term = dot_nn(w_in_ref[:, cut], grad_pre)
        grad = term if grad is None else grad + term
    grad_ref[...] = grad + cot.astype(F32).T
    shared = (grad * inv).astype(BF)
    shared_ref[...] = shared
    back = dot_nt(shared, mat_ref[...])

    @pl.when(step == 0)
    def _():
        acc_ref[...] = back

    @pl.when(step > 0)
    def _():
        acc_ref[...] += back

    @pl.when(step == NY - 1)
    def _():
        back_ref[...] = acc_ref[...].astype(BF)


def mlp(total, received, mat, hidden, count, cot, w_in_t, w_in, w_out):
    hid, targets = hidden.shape
    inner = w_in.shape[1]
    halo = received.shape[1]
    tile = pl.BlockSpec((hid, BLOCK), lambda i: (0, i))
    return pl.pallas_call(
        mlp_body,
        grid=(NY,),
        in_specs=[
            tile,
            whole((hid, halo)),
            pl.BlockSpec((halo, BLOCK), lambda i: (0, i)),
            tile,
            pl.BlockSpec((1, BLOCK), lambda i: (0, i)),
            pl.BlockSpec((BLOCK, hid), lambda i: (i, 0)),
            whole((inner, hid)),
            whole((hid, inner)),
            whole((inner, hid)),
        ],
        out_specs=[whole((hid, BLOCK)), tile, tile, whole((hid, halo))],
        out_shape=[
            jax.ShapeDtypeStruct((hid, BLOCK), BF),
            jax.ShapeDtypeStruct((hid, targets), F32),
            jax.ShapeDtypeStruct((hid, targets), BF),
            jax.ShapeDtypeStruct((hid, halo), BF),
        ],
        scratch_shapes=[pltpu.VMEM((hid, halo), F32)],
        cost_estimate=cost(4 * hid * targets * (inner + halo), 20 << 20),
        compiler_params=grant(20),
        name="mlp",
    )(total, received, mat, hidden, count, cot, w_in_t, w_in, w_out)


def last_body(core_ref, part_ref, returned_ref, pick_ref, *refs):
    pre_refs, agg_refs = refs[:NY], refs[NY : 2 * NY]
    keep_ref, give_ref, acc_ref = refs[2 * NY :]
    total = None
    for d in range(NY):
        cut = slice(BLOCK * d, BLOCK * (d + 1))
        grad = part_ref[:, cut] + dot_nt(returned_ref[...], pick_ref[cut, :])
        grad = (grad * slope(pre_refs[d][...].astype(F32))).astype(BF)
        term = dot_nt(agg_refs[d][...], grad)
        total = term if total is None else total + term
    acc_ref[...] = total
    half = keep_ref.shape[0]
    core = core_ref[0]
    keep_ref[...] = acc_ref[pl.ds(pl.multiple_of(core * half, half), half), :]
    give_ref[...] = acc_ref[pl.ds(pl.multiple_of((1 - core) * half, half), half), :]


def last(core, part, returned, pick, pre, agg):
    feats = agg[0].shape[0]
    hid = part.shape[0]
    out = jax.ShapeDtypeStruct((feats // 2, hid), F32)
    spec = pltpu.PrefetchScalarGridSpec(
        num_scalar_prefetch=1,
        grid=(1,),
        in_specs=[whole(v.shape) for v in (part, returned, pick, *pre, *agg)],
        out_specs=[whole(out.shape)] * 2,
        scratch_shapes=[pltpu.VMEM((feats, hid), F32)],
    )
    return pl.pallas_call(
        last_body, grid_spec=spec, out_shape=[out, out],
        cost_estimate=cost(4 << 30, 8 << 20), compiler_params=grant(16),
        name="last",
    )(core, part, returned, pick, *pre, *agg)


def shift(value, axis, by):
    devices = lax.axis_size(axis)
    return lax.ppermute(value, axis, [(i, (i + by) % devices) for i in range(devices)])


def swap(value, axis, bit):
    return lax.ppermute(value, axis, [(i, i ^ bit) for i in range(lax.axis_size(axis))])


def gather_z(piece):
    wide = jnp.broadcast_to(piece[None], (NZ,) + piece.shape)
    return lax.all_to_all(wide, "z", 0, 0).reshape(NZ * piece.shape[0], piece.shape[1])


def gather_y(own):
    return [own] + [shift(own, "y", NY - d) for d in range(1, NY)]


def body(
    face_grid,
    first_nbrs,
    first_count,
    w_first,
    b_first,
    send_rows,
    second_nbrs,
    second_count,
    w_in,
    w_out,
    out_grad,
):
    y, z = lax.axis_index("y"), lax.axis_index("z")
    core = lax.axis_index("core").astype(jnp.int32)
    targets = first_nbrs.shape[0]
    hid = w_first.shape[1]
    halo = send_rows.shape[0]

    inputs = [face_grid.T, first_nbrs.T, first_count[None, :], w_first]
    agg, got = {}, []
    for group in ((2,), (1, 3), (0,)):
        blocks = jnp.stack([((y + d) & (NY - 1)).astype(jnp.int32) for d in group])
        out = agg_chunk(blocks, inputs)
        for i, d in enumerate(group):
            agg[d], part = out[2 * i : 2 * i + 2]
            got.append(part if d == 0 else shift(part, "y", d))
    other = swap(out_grad, "z", 1)
    odd, second, third = (((z >> bit) & 1) == 1 for bit in range(3))
    pair = jnp.concatenate([out_grad, other], axis=0)
    pair = jnp.where(odd, jnp.concatenate([other, out_grad], axis=0), pair)
    others = [swap(pair, "z", bits) for bits in (2, 4, 6)]
    cot = jnp.stack([pair, *others]).reshape(2, 2, *pair.shape)
    cot = jnp.where(second, cot[:, ::-1], cot)
    cot = jnp.where(third, cot[::-1], cot).reshape(BLOCK, hid)

    lists = pack(second_nbrs.T, second_count[None, :])
    part_y = sum(g.astype(F32) for g in got).astype(BF).reshape(NZ, hid // NZ, BLOCK)
    part_y = jnp.concatenate(
        [part_y, jnp.broadcast_to(lists[None], (NZ,) + lists.shape)], axis=1
    )
    by_z = lax.all_to_all(part_y, "z", 0, 0)
    lists, by_z = by_z[:, hid // NZ :, : BLOCK // 2], by_z[:, : hid // NZ]
    bias = lax.dynamic_slice(b_first, (z * (hid // NZ),), (hid // NZ,))
    pre_own = (jnp.sum(by_z.astype(F32), axis=0) + bias[:, None]).astype(BF)
    pre = gather_z(pre_own)
    pre = gather_y(pre)

    lists = gather_y(lists)
    cot = gather_y(cot)
    nbrs2, count2 = unpack(y.astype(jnp.int32).reshape(1), lists)
    mat = count_matrix(nbrs2, count2, 0, targets)
    mat_halo = count_matrix(nbrs2, count2, targets, halo)
    cot = jnp.concatenate(cot, axis=0)
    rows = ((send_rows - y * BLOCK) & (targets - 1))[None, :]
    pick = count_matrix(rows, jnp.ones_like(rows), 0, targets)

    hidden = jax.nn.silu(jnp.concatenate(pre, axis=1).astype(F32)).astype(BF)
    received = shift(dot_nn(hidden, pick).astype(BF), ("x", "core"), 1)
    total = dot_nn(hidden, mat)
    agg2, grad_agg, shared, back = mlp(
        total, received, mat_halo, hidden, count2, cot, w_in.T, w_in, w_out
    )
    returned = shift(back, ("x", "core"), -1)
    grad_part = grad_agg + dot_nt(shared, mat)

    first = z * (BLOCK // NZ)
    own_agg = lax.dynamic_slice(agg2, (0, first), (hid, BLOCK // NZ))
    own_hidden = lax.dynamic_slice(hidden, (0, first), (hid, BLOCK // NZ))
    act = jax.nn.silu(dot_tn(own_agg, w_in)).astype(BF)
    embed = (own_hidden.T.astype(F32) + dot_nn(act, w_out)).astype(BF)

    keep, give = last(core.reshape(1), grad_part, returned, pick, pre, [agg[d] for d in range(NY)])
    pair = (keep + swap(give, "core", 1)).astype(BF)
    one, two, three = (swap(pair, "x", bit).astype(F32) for bit in (1, 2, 3))
    done = (pair.astype(F32) + one) + (two + three)
    done, embed = lax.optimization_barrier((done, embed))
    other = swap(done, "core", 1)
    grad_first = jnp.concatenate(
        [jnp.where(core == 0, done, other), jnp.where(core == 0, other, done)], axis=0
    )
    return embed, grad_first


def solution(mesh):
    fine = Mesh(mesh.devices.reshape(NY, NZ, 4, 2), ("y", "z", "x", "core"))
    feat, dp, every = ("y", "z"), ("x", "core"), ("x", "core", "y", "z")

    return jax.shard_map(
        body,
        mesh=fine,
        in_specs=(
            P(dp, feat),
            P(dp, None),
            P(dp),
            P(feat, None),
            P(),
            P(dp),
            P(every, None),
            P(every),
            P(),
            P(),
            P(every, None),
        ),
        out_specs=(P(every, None), P(feat, None)),
        check_vma=False,
    )
```

```python
import functools

import jax
import jax.numpy as jnp
from jax import lax
from jax.experimental import pallas as pl
from jax.experimental.pallas import tpu as pltpu
from jax.sharding import Mesh, PartitionSpec as P


BF = jnp.bfloat16
F32 = jnp.float32
NY, NZ = 4, 8
BLOCK = 512
PIECE = BLOCK // NZ


def dot_nn(a, b):
    return lax.dot_general(a, b, (((1,), (0,)), ((), ())), preferred_element_type=F32)


def dot_nt(a, b):
    return lax.dot_general(a, b, (((1,), (1,)), ((), ())), preferred_element_type=F32)


def dot_tn(a, b):
    return lax.dot_general(a, b, (((0,), (0,)), ((), ())), preferred_element_type=F32)


def slope(value):
    half = 0.5 * jnp.tanh(0.5 * value)
    sig = 0.5 + half
    return sig * (1.0 + value * (0.5 - half))


def live_slots(nbrs, count):
    slot = lax.broadcasted_iota(jnp.int32, nbrs.shape, 0)
    idx = jnp.where(slot < count, nbrs, -1).astype(F32)
    mult = sum(jnp.where(idx == idx[k : k + 1], 1.0, 0.0) for k in range(nbrs.shape[0]))
    return idx, mult


def count_rows(idx, mult, base, rows):
    slots, width = idx.shape
    local = idx - base
    cols = [jnp.broadcast_to(local[k : k + 1, :], (16, width)).astype(BF) for k in range(slots)]
    vals = [jnp.broadcast_to(mult[k : k + 1, :], (16, width)).astype(BF) for k in range(slots)]
    row = lax.broadcasted_iota(jnp.int32, (16, width), 0).astype(F32)
    out = []
    for group in range(rows // 16):
        here = (row + float(16 * group)).astype(BF)
        acc = jnp.zeros((16, width), BF)
        for k in range(slots):
            acc = jnp.where(here == cols[k], vals[k], acc)
        out.append(acc)
    return jnp.concatenate(out, axis=0)


def whole(shape):
    return pl.BlockSpec(shape, lambda *_: (0,) * len(shape))


def grant(mib):
    return pltpu.CompilerParams(vmem_limit_bytes=mib << 20)


def cost(flops, moved):
    return pl.CostEstimate(flops=flops, bytes_accessed=moved, transcendentals=0)


def aggregate(block, face_ref, nbrs, count, w, ready, agg_ref, part_ref, looped):
    width = agg_ref.shape[1]
    idx, mult = live_slots(nbrs, count)
    total = jnp.zeros(agg_ref.shape, F32)
    loops, size = (2, face_ref.shape[1] // 2) if looped else (1, face_ref.shape[1])

    def some(h, total):
        for at in range(0, size, 256):
            base = h * size + at
            counts = count_rows(idx, mult, (base + jnp.int32(0)).astype(F32), 256)
            ready(base, at)
            faces = face_ref[:, pl.ds(pl.multiple_of(base, 256), 256)]
            total = total + dot_nn(faces, counts)
        return total

    total = lax.fori_loop(0, loops, some, total) if looped else some(0, total)
    start = pl.multiple_of(block * width, width)
    own = face_ref[:, pl.ds(start, width)].astype(F32)
    agg = (own + total * (1.0 / count.astype(F32))).astype(BF)
    agg_ref[...] = agg
    part_ref[...] = dot_tn(w, agg).astype(BF)


PIECES = 4


def chunk_body(y_ref, face_hbm, nbrs_hbm, count_hbm, w_hbm, *refs, group):
    outs, (face_ref, nbrs_ref, count_ref, w_ref, sems) = refs[:-5], refs[-5:]
    width = face_ref.shape[1] // PIECES
    small = [
        pltpu.make_async_copy(nbrs_hbm, nbrs_ref, sems.at[PIECES]),
        pltpu.make_async_copy(count_hbm, count_ref, sems.at[PIECES + 1]),
        pltpu.make_async_copy(w_hbm, w_ref, sems.at[PIECES + 2]),
    ]

    def big(i):
        cut = pl.ds(pl.multiple_of(i * width, width), width)
        return pltpu.make_async_copy(face_hbm.at[:, cut], face_ref.at[:, cut], sems.at[i])

    for copy in small + [big(p) for p in range(PIECES)]:
        copy.start()
    for copy in small:
        copy.wait()

    for i, d in enumerate(group):

        def ready(base, at):
            if i == 0 and at % width == 0:
                big(base // width).wait()

        block = (y_ref[0] + d) & (NY - 1)
        cut = pl.ds(pl.multiple_of(block * BLOCK, BLOCK), BLOCK)
        aggregate(
            block, face_ref, nbrs_ref[:, cut], count_ref[:, cut], w_ref[...], ready,
            outs[2 * i], outs[2 * i + 1], len(group) == 1,
        )


def agg_chunk(y, inputs, group):
    feats, hid = inputs[3].shape
    out = [((feats, BLOCK), BF), ((hid, BLOCK), BF)] * len(group)
    spec = pltpu.PrefetchScalarGridSpec(
        num_scalar_prefetch=1,
        grid=(1,),
        in_specs=[pl.BlockSpec(memory_space=pltpu.HBM)] * len(inputs),
        out_specs=[whole(shape) for shape, _ in out],
        scratch_shapes=[pltpu.VMEM(v.shape, v.dtype) for v in inputs]
        + [pltpu.SemaphoreType.DMA((PIECES + 3,))],
    )
    work = 2 * BLOCK * feats * (inputs[0].shape[1] + hid) * len(group)
    return pl.pallas_call(
        functools.partial(chunk_body, group=group),
        grid_spec=spec,
        out_shape=[jax.ShapeDtypeStruct(*v) for v in out],
        compiler_params=grant(60),
        cost_estimate=cost(work, 4 << 20),
        name="agg_chunk",
    )(y, *inputs)


def count_body(nbrs_ref, count_ref, out_ref, *, first):
    rows, width = out_ref.shape
    base = (first + pl.program_id(0) * rows).astype(F32)

    def step(c, carry):
        cut = pl.ds(pl.multiple_of(c * BLOCK, BLOCK), BLOCK)
        idx, mult = live_slots(nbrs_ref[:, cut], count_ref[:, cut])
        out_ref[:, cut] = count_rows(idx, mult, base, rows)
        return carry

    lax.fori_loop(0, width // BLOCK, step, 0)


def count_matrix(nbrs, count, first, rows, mib=12, step=256):
    slots, width = nbrs.shape
    return pl.pallas_call(
        functools.partial(count_body, first=first),
        grid=(rows // step,),
        in_specs=[whole((slots, width)), whole((1, width))],
        out_specs=pl.BlockSpec((step, width), lambda i: (i, 0)),
        out_shape=jax.ShapeDtypeStruct((rows, width), BF),
        compiler_params=grant(mib),
        cost_estimate=cost(slots * rows * width * 200, 2 * rows * width),
        name="count_matrix",
    )(nbrs, count)


def pack_body(nbrs_ref, count_ref, out_ref):
    nbrs = nbrs_ref[...]
    count = jnp.broadcast_to(count_ref[...], nbrs.shape)
    rows = jnp.concatenate([nbrs >> 8, nbrs & 255, count, jnp.zeros_like(nbrs)], axis=1)
    rows = jnp.concatenate([rows, jnp.zeros_like(rows)], axis=0).astype(F32).astype(BF)
    out_ref[...] = jnp.concatenate([rows, jnp.zeros_like(rows)], axis=1)


def pack(nbrs_t, count):
    shape = (16, BLOCK)
    return pl.pallas_call(
        pack_body,
        in_specs=[whole(v.shape) for v in (nbrs_t, count)],
        out_specs=whole(shape),
        grid=(1,),
        out_shape=jax.ShapeDtypeStruct(shape, BF),
        compiler_params=grant(12),
        name="pack",
    )(nbrs_t, count)


def unpack_body(y_ref, *refs):
    nbrs_ref, count_ref = refs[NY:]
    targets = nbrs_ref.shape[1]
    nbrs, count = [], []
    for d in range(NY):
        for z in range(NZ):
            rows = refs[d][z].astype(F32)[:8].astype(jnp.int32)
            nbrs.append(rows[:, :PIECE] * 256 + rows[:, PIECE : 2 * PIECE])
            count.append(rows[0:1, 2 * PIECE : 3 * PIECE])
    nbrs = jnp.concatenate(nbrs, axis=1)
    turned = (nbrs - y_ref[0] * BLOCK) & (targets - 1)
    nbrs_ref[...] = jnp.where(nbrs < targets, turned, nbrs)
    count_ref[...] = jnp.concatenate(count, axis=1)


def unpack(y, blocks):
    targets = NY * NZ * PIECE
    out = [((8, targets), jnp.int32), ((1, targets), jnp.int32)]
    spec = pltpu.PrefetchScalarGridSpec(
        num_scalar_prefetch=1,
        grid=(1,),
        in_specs=[whole(v.shape) for v in blocks],
        out_specs=[whole(shape) for shape, _ in out],
    )
    return pl.pallas_call(
        unpack_body,
        grid_spec=spec,
        out_shape=[jax.ShapeDtypeStruct(*v) for v in out],
        compiler_params=grant(12),
        name="unpack",
    )(y, *blocks)


def mlp_body(
    total_ref, received_ref, mat_ref, hidden_ref, count_ref, cot_ref, w_in_t_ref, w_in_ref, w_out_ref,
    agg_ref, grad_ref, shared_ref, back_ref, acc_ref,
):
    step = pl.program_id(0)
    inv = 1.0 / count_ref[...].astype(F32)
    total = total_ref[...] + dot_nn(received_ref[...], mat_ref[...])
    agg = (hidden_ref[...].astype(F32) + total * inv).astype(BF)

    @pl.when(step == 0)
    def _():
        agg_ref[...] = agg

    cot = cot_ref[...]
    grad = None
    inner = w_in_ref.shape[1]
    for m in range(1):
        cut = slice(inner * m, inner * (m + 1))
        pre = dot_nn(w_in_t_ref[cut, :], agg)
        grad_act = dot_nt(w_out_ref[cut, :], cot)
        grad_pre = (grad_act * slope(pre)).astype(BF)
        term = dot_nn(w_in_ref[:, cut], grad_pre)
        grad = term if grad is None else grad + term
    grad_ref[...] = grad + cot.astype(F32).T
    shared = (grad * inv).astype(BF)
    shared_ref[...] = shared
    back = dot_nt(shared, mat_ref[...])

    @pl.when(step == 0)
    def _():
        acc_ref[...] = back

    @pl.when(step > 0)
    def _():
        acc_ref[...] += back

    @pl.when(step == NY - 1)
    def _():
        back_ref[...] = acc_ref[...].astype(BF)


def mlp(total, received, mat, hidden, count, cot, w_in_t, w_in, w_out):
    hid, targets = hidden.shape
    inner = w_in.shape[1]
    halo = received.shape[1]
    tile = pl.BlockSpec((hid, BLOCK), lambda i: (0, i))
    return pl.pallas_call(
        mlp_body,
        grid=(NY,),
        in_specs=[
            tile,
            whole((hid, halo)),
            pl.BlockSpec((halo, BLOCK), lambda i: (0, i)),
            tile,
            pl.BlockSpec((1, BLOCK), lambda i: (0, i)),
            pl.BlockSpec((BLOCK, hid), lambda i: (i, 0)),
            whole((inner, hid)),
            whole((hid, inner)),
            whole((inner, hid)),
        ],
        out_specs=[whole((hid, BLOCK)), tile, tile, whole((hid, halo))],
        out_shape=[
            jax.ShapeDtypeStruct((hid, BLOCK), BF),
            jax.ShapeDtypeStruct((hid, targets), F32),
            jax.ShapeDtypeStruct((hid, targets), BF),
            jax.ShapeDtypeStruct((hid, halo), BF),
        ],
        scratch_shapes=[pltpu.VMEM((hid, halo), F32)],
        cost_estimate=cost(4 * hid * targets * (inner + halo), 20 << 20),
        compiler_params=grant(20),
        name="mlp",
    )(total, received, mat, hidden, count, cot, w_in_t, w_in, w_out)


def last_body(core_ref, part_ref, returned_ref, pick_ref, *refs):
    pre_refs, agg_refs = refs[:NY], refs[NY : 2 * NY]
    keep_ref, give_ref, acc_ref = refs[2 * NY :]
    total = None
    for d in range(NY):
        cut = slice(BLOCK * d, BLOCK * (d + 1))
        grad = part_ref[:, cut] + dot_nt(returned_ref[...], pick_ref[cut, :])
        grad = (grad * slope(pre_refs[d][...].astype(F32))).astype(BF)
        term = dot_nt(agg_refs[d][...], grad)
        total = term if total is None else total + term
    acc_ref[...] = total
    half = keep_ref.shape[0]
    core = core_ref[0]
    keep_ref[...] = acc_ref[pl.ds(pl.multiple_of(core * half, half), half), :]
    give_ref[...] = acc_ref[pl.ds(pl.multiple_of((1 - core) * half, half), half), :]


def last(core, part, returned, pick, pre, agg):
    feats = agg[0].shape[0]
    hid = part.shape[0]
    out = jax.ShapeDtypeStruct((feats // 2, hid), F32)
    spec = pltpu.PrefetchScalarGridSpec(
        num_scalar_prefetch=1,
        grid=(1,),
        in_specs=[whole(v.shape) for v in (part, returned, pick, *pre, *agg)],
        out_specs=[whole(out.shape)] * 2,
        scratch_shapes=[pltpu.VMEM((feats, hid), F32)],
    )
    return pl.pallas_call(
        last_body, grid_spec=spec, out_shape=[out, out],
        cost_estimate=cost(4 << 30, 8 << 20), compiler_params=grant(16),
        name="last",
    )(core, part, returned, pick, *pre, *agg)


def shift(value, axis, by):
    devices = lax.axis_size(axis)
    return lax.ppermute(value, axis, [(i, (i + by) % devices) for i in range(devices)])


def swap(value, axis, bit):
    return lax.ppermute(value, axis, [(i, i ^ bit) for i in range(lax.axis_size(axis))])


def gather_z(piece):
    wide = jnp.broadcast_to(piece[None], (NZ,) + piece.shape)
    return lax.all_to_all(wide, "z", 0, 0).reshape(NZ * piece.shape[0], piece.shape[1])


def gather_y(own):
    return [own] + [shift(own, "y", NY - d) for d in range(1, NY)]


def body(
    face_grid,
    first_nbrs,
    first_count,
    w_first,
    b_first,
    send_rows,
    second_nbrs,
    second_count,
    w_in,
    w_out,
    out_grad,
):
    y, z = lax.axis_index("y"), lax.axis_index("z")
    core = lax.axis_index("core").astype(jnp.int32)
    targets = first_nbrs.shape[0]
    hid = w_first.shape[1]
    halo = send_rows.shape[0]

    inputs = [face_grid.T, first_nbrs.T, first_count[None, :], w_first]
    y_ref = y.astype(jnp.int32).reshape(1)
    agg, got = {}, []
    for group in ((2,), (1, 3), (0,)):
        out = agg_chunk(y_ref, inputs, group)
        for i, d in enumerate(group):
            agg[d], part = out[2 * i : 2 * i + 2]
            got.append(part if d == 0 else shift(part, "y", d))
    other = swap(out_grad, "z", 1)
    odd, second, third = (((z >> bit) & 1) == 1 for bit in range(3))
    pair = jnp.concatenate([out_grad, other], axis=0)
    pair = jnp.where(odd, jnp.concatenate([other, out_grad], axis=0), pair)
    others = [swap(pair, "z", bits) for bits in (2, 4, 6)]
    cot = jnp.stack([pair, *others]).reshape(2, 2, *pair.shape)
    cot = jnp.where(second, cot[:, ::-1], cot)
    cot = jnp.where(third, cot[::-1], cot).reshape(BLOCK, hid)

    lists = pack(second_nbrs.T, second_count[None, :])
    part_y = sum(g.astype(F32) for g in got).astype(BF).reshape(NZ, hid // NZ, BLOCK)
    part_y = jnp.concatenate(
        [part_y, jnp.broadcast_to(lists[None], (NZ,) + lists.shape)], axis=1
    )
    by_z = lax.all_to_all(part_y, "z", 0, 0)
    lists, by_z = by_z[:, hid // NZ :, : BLOCK // 2], by_z[:, : hid // NZ]
    bias = lax.dynamic_slice(b_first, (z * (hid // NZ),), (hid // NZ,))
    pre_own = (jnp.sum(by_z.astype(F32), axis=0) + bias[:, None]).astype(BF)
    pre = gather_z(pre_own)
    pre = gather_y(pre)

    lists = gather_y(lists)
    cot = gather_y(cot)
    nbrs2, count2 = unpack(y_ref, lists)
    mat = count_matrix(nbrs2, count2, 0, targets)
    mat_halo = count_matrix(nbrs2, count2, targets, halo)
    cot = jnp.concatenate(cot, axis=0)
    rows = ((send_rows - y * BLOCK) & (targets - 1))[None, :]
    pick = count_matrix(rows, jnp.ones_like(rows), 0, targets)

    hidden = jax.nn.silu(jnp.concatenate(pre, axis=1).astype(F32)).astype(BF)
    received = shift(dot_nn(hidden, pick).astype(BF), ("x", "core"), 1)
    total = dot_nn(hidden, mat)
    agg2, grad_agg, shared, back = mlp(
        total, received, mat_halo, hidden, count2, cot, w_in.T, w_in, w_out
    )
    returned = shift(back, ("x", "core"), -1)
    grad_part = grad_agg + dot_nt(shared, mat)

    first = z * (BLOCK // NZ)
    own_agg = lax.dynamic_slice(agg2, (0, first), (hid, BLOCK // NZ))
    own_hidden = lax.dynamic_slice(hidden, (0, first), (hid, BLOCK // NZ))
    act = jax.nn.silu(dot_tn(own_agg, w_in)).astype(BF)
    embed = (own_hidden.T.astype(F32) + dot_nn(act, w_out)).astype(BF)

    keep, give = last(core.reshape(1), grad_part, returned, pick, pre, [agg[d] for d in range(NY)])
    pair = (keep + swap(give, "core", 1)).astype(BF)
    one, two, three = (swap(pair, "x", bit).astype(F32) for bit in (1, 2, 3))
    done = (pair.astype(F32) + one) + (two + three)
    done, embed = lax.optimization_barrier((done, embed))
    other = swap(done, "core", 1)
    grad_first = jnp.concatenate(
        [jnp.where(core == 0, done, other), jnp.where(core == 0, other, done)], axis=0
    )
    return embed, grad_first


def solution(mesh):
    fine = Mesh(mesh.devices.reshape(NY, NZ, 4, 2), ("y", "z", "x", "core"))
    feat, dp, every = ("y", "z"), ("x", "core"), ("x", "core", "y", "z")

    return jax.shard_map(
        body,
        mesh=fine,
        in_specs=(
            P(dp, feat),
            P(dp, None),
            P(dp),
            P(feat, None),
            P(),
            P(dp),
            P(every, None),
            P(every),
            P(),
            P(),
            P(every, None),
        ),
        out_specs=(P(every, None), P(feat, None)),
        check_vma=False,
    )
```

```python
import functools

import jax
import jax.numpy as jnp
from jax import lax
from jax.experimental import pallas as pl
from jax.experimental.pallas import tpu as pltpu
from jax.sharding import Mesh, PartitionSpec as P


BF = jnp.bfloat16
F32 = jnp.float32
NY, NZ = 4, 8
BLOCK = 512
PIECE = BLOCK // NZ


def dot_nn(a, b):
    return lax.dot_general(a, b, (((1,), (0,)), ((), ())), preferred_element_type=F32)


def dot_nt(a, b):
    return lax.dot_general(a, b, (((1,), (1,)), ((), ())), preferred_element_type=F32)


def dot_tn(a, b):
    return lax.dot_general(a, b, (((0,), (0,)), ((), ())), preferred_element_type=F32)


def slope(value):
    half = 0.5 * jnp.tanh(0.5 * value)
    sig = 0.5 + half
    return sig * (1.0 + value * (0.5 - half))


def live_slots(nbrs, count):
    slot = lax.broadcasted_iota(jnp.int32, nbrs.shape, 0)
    idx = jnp.where(slot < count, nbrs, -1).astype(F32)
    mult = sum(jnp.where(idx == idx[k : k + 1], 1.0, 0.0) for k in range(nbrs.shape[0]))
    return idx, mult


def count_rows(idx, mult, base, rows):
    slots, width = idx.shape
    local = idx - base
    cols = [jnp.broadcast_to(local[k : k + 1, :], (16, width)).astype(BF) for k in range(slots)]
    vals = [jnp.broadcast_to(mult[k : k + 1, :], (16, width)).astype(BF) for k in range(slots)]
    row = lax.broadcasted_iota(jnp.int32, (16, width), 0).astype(F32)
    out = []
    for group in range(rows // 16):
        here = (row + float(16 * group)).astype(BF)
        acc = jnp.zeros((16, width), BF)
        for k in range(slots):
            acc = jnp.where(here == cols[k], vals[k], acc)
        out.append(acc)
    return jnp.concatenate(out, axis=0)


def whole(shape):
    return pl.BlockSpec(shape, lambda *_: (0,) * len(shape))


def grant(mib):
    return pltpu.CompilerParams(vmem_limit_bytes=mib << 20)


def cost(flops, moved):
    return pl.CostEstimate(flops=flops, bytes_accessed=moved, transcendentals=0)


def aggregate(block, face_ref, nbrs, count, w, ready, agg_ref, part_ref, looped):
    width = agg_ref.shape[1]
    idx, mult = live_slots(nbrs, count)
    total = jnp.zeros(agg_ref.shape, F32)
    loops, size = (2, face_ref.shape[1] // 2) if looped else (1, face_ref.shape[1])

    def some(h, total):
        for at in range(0, size, 256):
            base = h * size + at
            counts = count_rows(idx, mult, (base + jnp.int32(0)).astype(F32), 256)
            ready(base, at)
            faces = face_ref[:, pl.ds(pl.multiple_of(base, 256), 256)]
            total = total + dot_nn(faces, counts)
        return total

    total = lax.fori_loop(0, loops, some, total) if looped else some(0, total)
    start = pl.multiple_of(block * width, width)
    own = face_ref[:, pl.ds(start, width)].astype(F32)
    agg = (own + total * (1.0 / count.astype(F32))).astype(BF)
    agg_ref[...] = agg
    part_ref[...] = dot_tn(w, agg).astype(BF)


PIECES = 8


def chunk_body(y_ref, face_hbm, nbrs_hbm, count_hbm, w_hbm, *refs, group):
    outs, (face_ref, nbrs_ref, count_ref, w_ref, sems) = refs[:-5], refs[-5:]
    width = face_ref.shape[1] // PIECES
    small = [
        pltpu.make_async_copy(nbrs_hbm, nbrs_ref, sems.at[PIECES]),
        pltpu.make_async_copy(count_hbm, count_ref, sems.at[PIECES + 1]),
        pltpu.make_async_copy(w_hbm, w_ref, sems.at[PIECES + 2]),
    ]

    def big(i):
        cut = pl.ds(pl.multiple_of(i * width, width), width)
        return pltpu.make_async_copy(face_hbm.at[:, cut], face_ref.at[:, cut], sems.at[i])

    for copy in small + [big(p) for p in range(PIECES)]:
        copy.start()
    for copy in small:
        copy.wait()

    for i, d in enumerate(group):

        def ready(base, at):
            if i == 0 and at % width == 0:
                big(base // width).wait()

        block = (y_ref[0] + d) & (NY - 1)
        cut = pl.ds(pl.multiple_of(block * BLOCK, BLOCK), BLOCK)
        aggregate(
            block, face_ref, nbrs_ref[:, cut], count_ref[:, cut], w_ref[...], ready,
            outs[2 * i], outs[2 * i + 1], len(group) == 1,
        )


def agg_chunk(y, inputs, group):
    feats, hid = inputs[3].shape
    out = [((feats, BLOCK), BF), ((hid, BLOCK), BF)] * len(group)
    spec = pltpu.PrefetchScalarGridSpec(
        num_scalar_prefetch=1,
        grid=(1,),
        in_specs=[pl.BlockSpec(memory_space=pltpu.HBM)] * len(inputs),
        out_specs=[whole(shape) for shape, _ in out],
        scratch_shapes=[pltpu.VMEM(v.shape, v.dtype) for v in inputs]
        + [pltpu.SemaphoreType.DMA((PIECES + 3,))],
    )
    work = 2 * BLOCK * feats * (inputs[0].shape[1] + hid) * len(group)
    return pl.pallas_call(
        functools.partial(chunk_body, group=group),
        grid_spec=spec,
        out_shape=[jax.ShapeDtypeStruct(*v) for v in out],
        compiler_params=grant(60),
        cost_estimate=cost(work, 4 << 20),
        name="agg_chunk",
    )(y, *inputs)


def count_body(nbrs_ref, count_ref, out_ref, *, first):
    rows, width = out_ref.shape
    base = (first + pl.program_id(0) * rows).astype(F32)

    def step(c, carry):
        cut = pl.ds(pl.multiple_of(c * BLOCK, BLOCK), BLOCK)
        idx, mult = live_slots(nbrs_ref[:, cut], count_ref[:, cut])
        out_ref[:, cut] = count_rows(idx, mult, base, rows)
        return carry

    lax.fori_loop(0, width // BLOCK, step, 0)


def count_matrix(nbrs, count, first, rows, mib=12, step=256):
    slots, width = nbrs.shape
    return pl.pallas_call(
        functools.partial(count_body, first=first),
        grid=(rows // step,),
        in_specs=[whole((slots, width)), whole((1, width))],
        out_specs=pl.BlockSpec((step, width), lambda i: (i, 0)),
        out_shape=jax.ShapeDtypeStruct((rows, width), BF),
        compiler_params=grant(mib),
        cost_estimate=cost(slots * rows * width * 200, 2 * rows * width),
        name="count_matrix",
    )(nbrs, count)


def pack_body(nbrs_ref, count_ref, out_ref):
    nbrs = nbrs_ref[...]
    count = jnp.broadcast_to(count_ref[...], nbrs.shape)
    rows = jnp.concatenate([nbrs >> 8, nbrs & 255, count, jnp.zeros_like(nbrs)], axis=1)
    rows = jnp.concatenate([rows, jnp.zeros_like(rows)], axis=0).astype(F32).astype(BF)
    out_ref[...] = jnp.concatenate([rows, jnp.zeros_like(rows)], axis=1)


def pack(nbrs_t, count):
    shape = (16, BLOCK)
    return pl.pallas_call(
        pack_body,
        in_specs=[whole(v.shape) for v in (nbrs_t, count)],
        out_specs=whole(shape),
        grid=(1,),
        out_shape=jax.ShapeDtypeStruct(shape, BF),
        compiler_params=grant(12),
        name="pack",
    )(nbrs_t, count)


def unpack_body(y_ref, *refs):
    nbrs_ref, count_ref = refs[NY:]
    targets = nbrs_ref.shape[1]
    nbrs, count = [], []
    for d in range(NY):
        for z in range(NZ):
            rows = refs[d][z].astype(F32)[:8].astype(jnp.int32)
            nbrs.append(rows[:, :PIECE] * 256 + rows[:, PIECE : 2 * PIECE])
            count.append(rows[0:1, 2 * PIECE : 3 * PIECE])
    nbrs = jnp.concatenate(nbrs, axis=1)
    turned = (nbrs - y_ref[0] * BLOCK) & (targets - 1)
    nbrs_ref[...] = jnp.where(nbrs < targets, turned, nbrs)
    count_ref[...] = jnp.concatenate(count, axis=1)


def unpack(y, blocks):
    targets = NY * NZ * PIECE
    out = [((8, targets), jnp.int32), ((1, targets), jnp.int32)]
    spec = pltpu.PrefetchScalarGridSpec(
        num_scalar_prefetch=1,
        grid=(1,),
        in_specs=[whole(v.shape) for v in blocks],
        out_specs=[whole(shape) for shape, _ in out],
    )
    return pl.pallas_call(
        unpack_body,
        grid_spec=spec,
        out_shape=[jax.ShapeDtypeStruct(*v) for v in out],
        compiler_params=grant(12),
        name="unpack",
    )(y, *blocks)


def mlp_body(
    total_ref, received_ref, mat_ref, hidden_ref, count_ref, cot_ref, w_in_t_ref, w_in_ref, w_out_ref,
    agg_ref, grad_ref, shared_ref, back_ref, acc_ref,
):
    step = pl.program_id(0)
    inv = 1.0 / count_ref[...].astype(F32)
    total = total_ref[...] + dot_nn(received_ref[...], mat_ref[...])
    agg = (hidden_ref[...].astype(F32) + total * inv).astype(BF)

    @pl.when(step == 0)
    def _():
        agg_ref[...] = agg

    cot = cot_ref[...]
    grad = None
    inner = w_in_ref.shape[1]
    for m in range(1):
        cut = slice(inner * m, inner * (m + 1))
        pre = dot_nn(w_in_t_ref[cut, :], agg)
        grad_act = dot_nt(w_out_ref[cut, :], cot)
        grad_pre = (grad_act * slope(pre)).astype(BF)
        term = dot_nn(w_in_ref[:, cut], grad_pre)
        grad = term if grad is None else grad + term
    grad_ref[...] = grad + cot.astype(F32).T
    shared = (grad * inv).astype(BF)
    shared_ref[...] = shared
    back = dot_nt(shared, mat_ref[...])

    @pl.when(step == 0)
    def _():
        acc_ref[...] = back

    @pl.when(step > 0)
    def _():
        acc_ref[...] += back

    @pl.when(step == NY - 1)
    def _():
        back_ref[...] = acc_ref[...].astype(BF)


def mlp(total, received, mat, hidden, count, cot, w_in_t, w_in, w_out):
    hid, targets = hidden.shape
    inner = w_in.shape[1]
    halo = received.shape[1]
    tile = pl.BlockSpec((hid, BLOCK), lambda i: (0, i))
    return pl.pallas_call(
        mlp_body,
        grid=(NY,),
        in_specs=[
            tile,
            whole((hid, halo)),
            pl.BlockSpec((halo, BLOCK), lambda i: (0, i)),
            tile,
            pl.BlockSpec((1, BLOCK), lambda i: (0, i)),
            pl.BlockSpec((BLOCK, hid), lambda i: (i, 0)),
            whole((inner, hid)),
            whole((hid, inner)),
            whole((inner, hid)),
        ],
        out_specs=[whole((hid, BLOCK)), tile, tile, whole((hid, halo))],
        out_shape=[
            jax.ShapeDtypeStruct((hid, BLOCK), BF),
            jax.ShapeDtypeStruct((hid, targets), F32),
            jax.ShapeDtypeStruct((hid, targets), BF),
            jax.ShapeDtypeStruct((hid, halo), BF),
        ],
        scratch_shapes=[pltpu.VMEM((hid, halo), F32)],
        cost_estimate=cost(4 * hid * targets * (inner + halo), 20 << 20),
        compiler_params=grant(20),
        name="mlp",
    )(total, received, mat, hidden, count, cot, w_in_t, w_in, w_out)


def last_body(core_ref, part_ref, returned_ref, pick_ref, *refs):
    pre_refs, agg_refs = refs[:NY], refs[NY : 2 * NY]
    keep_ref, give_ref, acc_ref = refs[2 * NY :]
    total = None
    for d in range(NY):
        cut = slice(BLOCK * d, BLOCK * (d + 1))
        grad = part_ref[:, cut] + dot_nt(returned_ref[...], pick_ref[cut, :])
        grad = (grad * slope(pre_refs[d][...].astype(F32))).astype(BF)
        term = dot_nt(agg_refs[d][...], grad)
        total = term if total is None else total + term
    acc_ref[...] = total
    half = keep_ref.shape[0]
    core = core_ref[0]
    keep_ref[...] = acc_ref[pl.ds(pl.multiple_of(core * half, half), half), :]
    give_ref[...] = acc_ref[pl.ds(pl.multiple_of((1 - core) * half, half), half), :]


def last(core, part, returned, pick, pre, agg):
    feats = agg[0].shape[0]
    hid = part.shape[0]
    out = jax.ShapeDtypeStruct((feats // 2, hid), F32)
    spec = pltpu.PrefetchScalarGridSpec(
        num_scalar_prefetch=1,
        grid=(1,),
        in_specs=[whole(v.shape) for v in (part, returned, pick, *pre, *agg)],
        out_specs=[whole(out.shape)] * 2,
        scratch_shapes=[pltpu.VMEM((feats, hid), F32)],
    )
    return pl.pallas_call(
        last_body, grid_spec=spec, out_shape=[out, out],
        cost_estimate=cost(4 << 30, 8 << 20), compiler_params=grant(16),
        name="last",
    )(core, part, returned, pick, *pre, *agg)


def shift(value, axis, by):
    devices = lax.axis_size(axis)
    return lax.ppermute(value, axis, [(i, (i + by) % devices) for i in range(devices)])


def swap(value, axis, bit):
    return lax.ppermute(value, axis, [(i, i ^ bit) for i in range(lax.axis_size(axis))])


def gather_z(piece):
    wide = jnp.broadcast_to(piece[None], (NZ,) + piece.shape)
    return lax.all_to_all(wide, "z", 0, 0).reshape(NZ * piece.shape[0], piece.shape[1])


def gather_y(own):
    return [own] + [shift(own, "y", NY - d) for d in range(1, NY)]


def body(
    face_grid,
    first_nbrs,
    first_count,
    w_first,
    b_first,
    send_rows,
    second_nbrs,
    second_count,
    w_in,
    w_out,
    out_grad,
):
    y, z = lax.axis_index("y"), lax.axis_index("z")
    core = lax.axis_index("core").astype(jnp.int32)
    targets = first_nbrs.shape[0]
    hid = w_first.shape[1]
    halo = send_rows.shape[0]

    inputs = [face_grid.T, first_nbrs.T, first_count[None, :], w_first]
    y_ref = y.astype(jnp.int32).reshape(1)
    agg, got = {}, []
    for group in ((2,), (1, 3), (0,)):
        out = agg_chunk(y_ref, inputs, group)
        for i, d in enumerate(group):
            agg[d], part = out[2 * i : 2 * i + 2]
            got.append(part if d == 0 else shift(part, "y", d))
    other = swap(out_grad, "z", 1)
    odd, second, third = (((z >> bit) & 1) == 1 for bit in range(3))
    pair = jnp.concatenate([out_grad, other], axis=0)
    pair = jnp.where(odd, jnp.concatenate([other, out_grad], axis=0), pair)
    others = [swap(pair, "z", bits) for bits in (2, 4, 6)]
    cot = jnp.stack([pair, *others]).reshape(2, 2, *pair.shape)
    cot = jnp.where(second, cot[:, ::-1], cot)
    cot = jnp.where(third, cot[::-1], cot).reshape(BLOCK, hid)

    lists = pack(second_nbrs.T, second_count[None, :])
    part_y = sum(g.astype(F32) for g in got).astype(BF).reshape(NZ, hid // NZ, BLOCK)
    part_y = jnp.concatenate(
        [part_y, jnp.broadcast_to(lists[None], (NZ,) + lists.shape)], axis=1
    )
    by_z = lax.all_to_all(part_y, "z", 0, 0)
    lists, by_z = by_z[:, hid // NZ :, : BLOCK // 2], by_z[:, : hid // NZ]
    bias = lax.dynamic_slice(b_first, (z * (hid // NZ),), (hid // NZ,))
    pre_own = (jnp.sum(by_z.astype(F32), axis=0) + bias[:, None]).astype(BF)
    pre = gather_z(pre_own)
    pre = gather_y(pre)

    lists = gather_y(lists)
    cot = gather_y(cot)
    nbrs2, count2 = unpack(y_ref, lists)
    mat = count_matrix(nbrs2, count2, 0, targets)
    mat_halo = count_matrix(nbrs2, count2, targets, halo)
    cot = jnp.concatenate(cot, axis=0)
    rows = ((send_rows - y * BLOCK) & (targets - 1))[None, :]
    pick = count_matrix(rows, jnp.ones_like(rows), 0, targets)

    hidden = jax.nn.silu(jnp.concatenate(pre, axis=1).astype(F32)).astype(BF)
    received = shift(dot_nn(hidden, pick).astype(BF), ("x", "core"), 1)
    total = dot_nn(hidden, mat)
    agg2, grad_agg, shared, back = mlp(
        total, received, mat_halo, hidden, count2, cot, w_in.T, w_in, w_out
    )
    returned = shift(back, ("x", "core"), -1)
    grad_part = grad_agg + dot_nt(shared, mat)

    first = z * (BLOCK // NZ)
    own_agg = lax.dynamic_slice(agg2, (0, first), (hid, BLOCK // NZ))
    own_hidden = lax.dynamic_slice(hidden, (0, first), (hid, BLOCK // NZ))
    act = jax.nn.silu(dot_tn(own_agg, w_in)).astype(BF)
    embed = (own_hidden.T.astype(F32) + dot_nn(act, w_out)).astype(BF)

    keep, give = last(core.reshape(1), grad_part, returned, pick, pre, [agg[d] for d in range(NY)])
    pair = (keep + swap(give, "core", 1)).astype(BF)
    others = []
    for bit in (1, 2, 3):
        others.append(swap(pair, "x", bit))
    one, two, three = (other.astype(F32) for other in others)
    done = (pair.astype(F32) + one) + (two + three)
    done, embed = lax.optimization_barrier((done, embed))
    other = swap(done, "core", 1)
    grad_first = jnp.concatenate(
        [jnp.where(core == 0, done, other), jnp.where(core == 0, other, done)], axis=0
    )
    return embed, grad_first


def solution(mesh):
    fine = Mesh(mesh.devices.reshape(NY, NZ, 4, 2), ("y", "z", "x", "core"))
    feat, dp, every = ("y", "z"), ("x", "core"), ("x", "core", "y", "z")

    return jax.shard_map(
        body,
        mesh=fine,
        in_specs=(
            P(dp, feat),
            P(dp, None),
            P(dp),
            P(feat, None),
            P(),
            P(dp),
            P(every, None),
            P(every),
            P(),
            P(),
            P(every, None),
        ),
        out_specs=(P(every, None), P(feat, None)),
        check_vma=False,
    )
```
